32 devices in a mesh: lat: 4 (over y, x), lon: 8 (over z, core).
Axes of the slice: x: 2, y: 2, z: 4, core: 2. Of those that a mesh axis runs over, the one named last changes fastest.
Arguments:
- tokens: bfloat16 [16384, 1024], P(('lat', 'lon')), may hold values from -60 to 60
- dest_tile: int32 [16384], P(('lat', 'lon')), may hold values from 0 to 32, as said below
- slot_cell: int32 [32, 32, 16], P(('lat', 'lon')), may hold values from 0 to 512, as said below
- w_up: bfloat16 [1024, 4096], replicated, may hold values from -0.1875 to 0.1875
- w_down: bfloat16 [4096, 1024], replicated, may hold values from -0.09375 to 0.09375
- w_proj: bfloat16 [1024, 256], replicated, may hold values from -0.1875 to 0.1875
- w_conv: bfloat16 [3, 3, 256, 256], replicated, may hold values from -0.125 to 0.125
- cotangent: bfloat16 [512, 128, 256], P('lat', 'lon'), may hold values from -6 to 6
Outputs:
- decoded: bfloat16 [512, 128, 256], P('lat', 'lon')
- weight_grad: float32 [3, 3, 256, 256], P(None, None, None, 'lon')
- token_grad: bfloat16 [16384, 256], P(('lat', 'lon'))
The draws below stay inside these ranges and needn't reach their ends.
Inputs may be any that keep to these rules, and one draw needn't show every extreme that they name: `dest_tile`: within a shard the live slots come first and their tiles never decrease. The ocean cells of a tile, in raster order after those of all earlier tiles, are dealt to the shards in turn, so a shard holds a tile's ocean count divided by 32, rounded down or up, and at most 16 tokens for one tile; in every draw some tile is all ocean and receives 16 tokens from every shard. `slot_cell`: entry [d, s, k] names the cell of tile d that receives the token of shard s with dest_tile d and rank k among them, or 512 where shard s has no such token; each cell is named at most once, and the named cells are the tile's ocean cells.
All inputs are finite; a program needn't handle non-finite values.
Results may differ from the reference program's by a relative error of at most 0.0077.
Values may be sent and summed in bfloat16 or wider, within the bound.
No kernel may reach another device: no remote copies, remote signals or barrier semaphores. Data moves between devices by JAX's collectives and lax.ppermute only.
A program may use at most 128 MiB of HBM per device.

```python
import math
from functools import partial
import jax
import jax.numpy as jnp
from jax import lax

D = 1024
MLP = 4096
C = 256
TH = 64
TW = 8
TILES = 32
CELLS = 512
TOK_DEV = 512
CAP = 16
TOKENS = 16384
FINE_ROWS = 512
FINE_COLS = 128
N_LAT = 4
N_LON = 8


def layout_tables(key):
    base_key = jax.random.fold_in(key, 7)
    share_key, full_key, roll_key = jax.random.split(base_key, 3)
    ocean_share = jax.random.randint(share_key, (TILES,), 30, 101)
    full_tile = jax.random.randint(full_key, (), 0, TILES)
    ocean_share = jnp.where(jnp.arange(TILES, dtype=jnp.int32) == full_tile, 101, ocean_share)
    rolls = jax.random.randint(roll_key, (TILES, CELLS), 0, 100)
    ocean_mask = (rolls < ocean_share[:, None]).astype(jnp.int32)
    ocean_count = jnp.sum(ocean_mask, axis=1)
    offsets = jnp.cumsum(ocean_count) - ocean_count
    local_rank = jnp.cumsum(ocean_mask, axis=1) - 1
    global_rank = offsets[:, None] + local_rank
    source = jnp.where(ocean_mask == 1, global_rank % TILES, TILES)
    shard_slot = global_rank // TILES
    tile_rank = local_rank // TILES
    tile_ids = jnp.broadcast_to(jnp.arange(TILES, dtype=jnp.int32)[:, None], (TILES, CELLS))
    cell_ids = jnp.broadcast_to(jnp.arange(CELLS, dtype=jnp.int32)[None, :], (TILES, CELLS))
    dest_table = jnp.full((TILES, TOK_DEV), TILES, jnp.int32).at[source, shard_slot].set(tile_ids, mode='drop')
    cell_table = jnp.full((TILES, TILES, CAP), CELLS, jnp.int32).at[tile_ids, source, tile_rank].set(cell_ids, mode='drop')
    return (dest_table.reshape(TOKENS), cell_table)


def draw_dest_tile(key, part):
    return layout_tables(key)[0]


def draw_slot_cell(key, part):
    return layout_tables(key)[1]


def draw_tokens(key, part):
    row_key, col_key, base_key = jax.random.split(jax.random.fold_in(key, 11), 3)
    row_scale = jnp.exp(jax.random.uniform(row_key, (TOKENS, 1), jnp.float32, math.log(0.3), math.log(3.0)))
    col_scale = jnp.exp(jax.random.uniform(col_key, (1, D), jnp.float32, math.log(0.3), math.log(3.0)))
    values = jax.random.normal(base_key, (TOKENS, D), jnp.float32)
    values = jnp.clip(values, -6.0, 6.0)
    return (values * row_scale * col_scale).astype(jnp.bfloat16)


def with_spikes(result, rng, source, target, shards_of, factor):
    def block_of(position):
        return (jnp.arange(result.shape[position]) // (result.shape[position] // shards_of)).reshape((-1,) + (1,) * (result.ndim - 1 - position))

    first = jax.random.permutation(rng, shards_of)[block_of(target)]
    other_side = (block_of(target) + shards_of // 2) % shards_of
    return jnp.where((block_of(source) == first) | (block_of(source) == other_side), factor * result, result)


def level_of(key, extent, cuts, low, high):
    def one(dim, blocks):
        steps = jax.random.uniform(jax.random.fold_in(jax.random.fold_in(key, 6), dim), (blocks,), jnp.float32, low / len(cuts), high / len(cuts))
        return jnp.repeat(jnp.exp(steps), extent[dim] // blocks).reshape((-1,) + (1,) * (len(extent) - dim - 1))

    factor_of = one(*cuts[0])
    for cut in cuts[1:]:
        factor_of = factor_of * one(*cut)
    return factor_of


def noise(rng, extent, width, bound, cuts=(), kind=jnp.bfloat16):
    factor_of = level_of(rng, extent, cuts, -0.22, 0.18) if cuts else 1.0
    values = jax.random.normal(rng, extent, jnp.float32) * width * factor_of
    return jnp.minimum(jnp.maximum(values, -bound), bound).astype(kind)


def heavy_noise(rng, shape, width, bound, pieces, heavy, kind=jnp.bfloat16):
    array = width * jax.random.normal(rng, shape, jnp.float32)
    if pieces:
        array = array * level_of(rng, shape, pieces, -0.22, 0.18)
    return jnp.clip(with_spikes(array, jax.random.fold_in(rng, 3), *heavy), -bound, bound).astype(kind)


def setup_inputs(seed: int = 0) -> dict:
    seeds = jax.random.split(jax.random.key(seed), 9)
    tokens = draw_tokens(jax.random.fold_in(seeds[8], 71), 0)
    dest_tile = draw_dest_tile(jax.random.fold_in(seeds[8], 71), 0)
    slot_cell = draw_slot_cell(jax.random.fold_in(seeds[8], 71), 0)
    w_up = noise(seeds[3], (D, MLP), D ** -0.5, 0.1875)
    w_down = noise(seeds[4], (MLP, D), MLP ** -0.5, 0.09375)
    w_proj = noise(seeds[5], (D, C), D ** -0.5, 0.1875)
    w_conv = noise(seeds[6], (3, 3, C, C), (9 * C) ** -0.5, 0.125)
    cotangent = heavy_noise(seeds[7], (FINE_ROWS, FINE_COLS, C), 1.0, 6.0, ((0, 4), (1, 8)), (1, 2, 8, 2.0))
    return dict(tokens=tokens, dest_tile=dest_tile, slot_cell=slot_cell, w_up=w_up, w_down=w_down, w_proj=w_proj, w_conv=w_conv, cotangent=cotangent)


def encode(rows_in, w_up, w_down):
    values = rows_in.astype(jnp.float32)
    center = values - lax.optimization_barrier(jnp.mean(values, axis=1, keepdims=True))
    spread = lax.optimization_barrier(jnp.mean(center * center, axis=1, keepdims=True))
    normed = (center * lax.rsqrt(spread + 1e-05)).astype(jnp.bfloat16)
    inner_sum = jnp.dot(normed, w_up, preferred_element_type=jnp.float32)
    hidden = jax.nn.gelu(inner_sum, approximate=True).astype(jnp.bfloat16)
    return (values + jnp.dot(hidden, w_down, preferred_element_type=jnp.float32)).astype(jnp.bfloat16)

def periodic_pad(field_in):
    wrapped = jnp.concatenate([field_in[:, -1:], field_in, field_in[:, :1]], axis=1)
    zero_rim = jnp.zeros((1,) + wrapped.shape[1:], field_in.dtype)
    return jnp.concatenate([zero_rim, wrapped, zero_rim], axis=0)

def to_grid(tiled_in):
    depth = tiled_in.shape[-1]
    return tiled_in.reshape(N_LAT, N_LON, TH, TW, depth).transpose(0, 2, 1, 3, 4).reshape(N_LAT * TH, N_LON * TW, depth)

def to_tiles(grid_in):
    depth = grid_in.shape[-1]
    return grid_in.reshape(N_LAT, TH, N_LON, TW, depth).transpose(0, 2, 1, 3, 4).reshape(N_LAT * N_LON, TH * TW, depth)

def reference(tokens, dest_tile, slot_cell, w_up, w_down, w_proj, w_conv, cotangent):
    tile_count = N_LAT * N_LON
    shards = tokens.reshape(tile_count, TOK_DEV, D)

    def project_shard(rows_in):
        return jnp.dot(encode(rows_in, w_up, w_down), w_proj, preferred_element_type=jnp.float32).astype(jnp.bfloat16)
    features = lax.map(project_shard, shards)
    dest_rows = dest_tile.reshape(tile_count, TOK_DEV)
    positions = jnp.arange(TOK_DEV, dtype=jnp.int32)

    def rank_of(row_ids):
        same_dest = jnp.logical_and(row_ids[:, None] == row_ids[None, :], positions[None, :] < positions[:, None])
        return lax.optimization_barrier(jnp.sum(same_dest.astype(jnp.int32), axis=1)).astype(jnp.int32)
    token_rank = lax.map(rank_of, dest_rows)
    source_ids = jnp.broadcast_to(jnp.arange(tile_count, dtype=jnp.int32)[:, None], (tile_count, TOK_DEV))
    token_ids = jnp.broadcast_to(positions[None, :], (tile_count, TOK_DEV))
    slot_token = jnp.full((tile_count, tile_count + 1, CAP), TOK_DEV, jnp.int32)
    slot_token = slot_token.at[source_ids, dest_rows, token_rank].set(token_ids, mode='drop')[:, :tile_count]
    padded_features = jnp.concatenate([features, jnp.zeros((tile_count, 1, C), features.dtype)], axis=1)
    lead_ids = jnp.broadcast_to(jnp.arange(tile_count, dtype=jnp.int32)[:, None, None], (tile_count, tile_count, CAP))
    fetched = padded_features[lead_ids, slot_token]
    latent = jnp.zeros((tile_count, CELLS + 1, C), features.dtype)
    latent = latent.at[lead_ids, slot_cell].set(jnp.transpose(fetched, (1, 0, 2, 3)))[:, :CELLS]
    ocean_cells = jnp.zeros((tile_count, CELLS + 1, 1), jnp.float32).at[lead_ids, slot_cell].set(1.0)[:, :CELLS]
    latent_grid = to_grid(latent)
    wet_grid = to_grid(ocean_cells)
    fine_grid = jnp.repeat(jnp.repeat(latent_grid, 2, axis=0), 2, axis=1)
    wet_fine = jnp.repeat(jnp.repeat(wet_grid, 2, axis=0), 2, axis=1).reshape(-1, 1)
    fine_rows, fine_cols = (fine_grid.shape[0], fine_grid.shape[1])
    framed = periodic_pad(fine_grid)
    mixed_sum = jnp.zeros((fine_rows * fine_cols, C), jnp.float32)
    for row_tap in range(3):
        for col_tap in range(3):
            window = framed[row_tap:row_tap + fine_rows, col_tap:col_tap + fine_cols].reshape(-1, C)
            mixed_sum = mixed_sum + jnp.dot(window, w_conv[row_tap, col_tap], preferred_element_type=jnp.float32)
    activate = partial(jax.nn.gelu, approximate=True)
    activated, pullback = jax.vjp(activate, mixed_sum)
    decoded = (wet_fine * activated).astype(jnp.bfloat16).reshape(fine_rows, fine_cols, C)
    adjoint = pullback(wet_fine * cotangent.reshape(-1, C).astype(jnp.float32))[0].astype(jnp.bfloat16)
    grad_scale = 1.0 / math.sqrt(fine_rows * fine_cols)
    tap_grads = []
    for row_tap in range(3):
        for col_tap in range(3):
            window = framed[row_tap:row_tap + fine_rows, col_tap:col_tap + fine_cols].reshape(-1, C)
            tap_grads.append(lax.dot_general(window, adjoint, (((0,), (0,)), ((), ())), preferred_element_type=jnp.float32))
    weight_grad = jnp.stack(tap_grads).reshape(3, 3, C, C) * grad_scale
    framed_adj = periodic_pad(adjoint.reshape(fine_rows, fine_cols, C))
    fine_grad = jnp.zeros((fine_rows * fine_cols, C), jnp.float32)
    for row_tap in range(3):
        for col_tap in range(3):
            window = framed_adj[2 - row_tap:2 - row_tap + fine_rows, 2 - col_tap:2 - col_tap + fine_cols].reshape(-1, C)
            fine_grad = fine_grad + lax.dot_general(window, w_conv[row_tap, col_tap], (((1,), (1,)), ((), ())), preferred_element_type=jnp.float32)
    cell_grad = fine_grad.reshape(fine_rows // 2, 2, fine_cols // 2, 2, C).sum(axis=(1, 3)).astype(jnp.bfloat16)
    tiled_grad = to_tiles(cell_grad)
    padded_grad = jnp.concatenate([tiled_grad, jnp.zeros((tile_count, 1, C), tiled_grad.dtype)], axis=1)
    returned = padded_grad[lead_ids, slot_cell]
    token_grad = jnp.zeros((tile_count, TOK_DEV + 1, C), jnp.bfloat16)
    token_grad = token_grad.at[lead_ids, slot_token].set(jnp.transpose(returned, (1, 0, 2, 3)))[:, :TOK_DEV]
    return (decoded, weight_grad, token_grad.reshape(TOKENS, C))
```

```python
from functools import partial
import math

import jax
import jax.numpy as jnp
from jax import lax
from jax.experimental import pallas as pl
from jax.experimental.pallas import tpu as pltpu
from jax.sharding import PartitionSpec as P

F32 = jnp.float32
BF16 = jnp.bfloat16
GELU_C = math.sqrt(2.0 / math.pi)
GELU_K = 0.044715


def pick(x, index, axis):
    return lax.dynamic_index_in_dim(x, index, axis, keepdims=False)


def shifted(axis, step):
    count = lax.axis_size(axis)
    return [(i, (i + step) % count) for i in range(count)]


def in_hbm(x):
    return pltpu.with_memory_space_constraint(x, pltpu.HBM)


def encode_kernel(
    tokens_ref, select_ref, proj_ref, up_ref, down_ref, out_ref, normed, hidden, total,
):
    step = pl.program_id(0)
    last = pl.num_programs(0) - 1

    @pl.when(step == 0)
    def _():
        values = tokens_ref[...].astype(F32)
        center = values - jnp.mean(values, axis=1, keepdims=True)
        spread = jnp.mean(center * center, axis=1, keepdims=True)
        normed[...] = (center * lax.rsqrt(spread + 1e-05)).astype(BF16)
        total[...] = values

    def grow(slot):
        inner = jnp.dot(normed[...], up_ref[...], preferred_element_type=F32)
        hidden[slot] = jax.nn.gelu(inner, approximate=True).astype(BF16)

    def shrink(slot):
        total[...] += jnp.dot(hidden[slot], down_ref[...], preferred_element_type=F32)

    @pl.when(step == 0)
    def _():
        grow(0)

    @pl.when(jnp.logical_and(step > 0, step < last))
    def _():
        shrink((step - 1) % 2)
        grow(step % 2)

    @pl.when(step == last)
    def _():
        shrink((step - 1) % 2)
        encoded = total[...].astype(BF16)
        features = jnp.dot(encoded, proj_ref[...], preferred_element_type=F32).astype(BF16)
        out_ref[...] = jnp.dot(select_ref[...], features, preferred_element_type=F32).astype(BF16)


def encode(tokens, selector, w_proj, w_up, w_down):
    count, width = tokens.shape
    inner = w_up.shape[1]
    chan = w_proj.shape[1]
    slots = selector.shape[0]
    chunk = 512
    steps = inner // chunk
    return pl.pallas_call(
        encode_kernel,
        grid=(steps + 1,),
        out_shape=jax.ShapeDtypeStruct((slots, chan), BF16),
        in_specs=[
            pl.BlockSpec((count, width), lambda j: (0, 0)),
            pl.BlockSpec((slots, count), lambda j: (0, 0)),
            pl.BlockSpec((width, chan), lambda j: (0, 0)),
            pl.BlockSpec((width, chunk), lambda j: (0, jnp.minimum(j, steps - 1))),
            pl.BlockSpec((chunk, width), lambda j: (jnp.maximum(j - 1, 0), 0)),
        ],
        out_specs=pl.BlockSpec((slots, chan), lambda j: (0, 0)),
        scratch_shapes=[
            pltpu.VMEM((count, width), BF16),
            pltpu.VMEM((2, count, chunk), BF16),
            pltpu.VMEM((count, width), F32),
        ],
        compiler_params=pltpu.CompilerParams(vmem_limit_bytes=40 * 1024 * 1024),
        name="encode",
    )(in_hbm(tokens), selector, *map(in_hbm, (w_proj, w_up, w_down)))


def rim_lat(top_edge, bottom_edge):
    place = lax.axis_index("lat")
    above = lax.ppermute(bottom_edge, "lat", shifted("lat", 1))
    below = lax.ppermute(top_edge, "lat", shifted("lat", -1))
    above = jnp.where(place == 0, jnp.zeros_like(above), above)
    below = jnp.where(place == lax.axis_size("lat") - 1, jnp.zeros_like(below), below)
    return above, below


def rim_lon(first, last):
    left = lax.ppermute(last, "lon", shifted("lon", 1))
    right = lax.ppermute(first, "lon", shifted("lon", -1))
    return left, right


def weights_kernel(conv_ref, vertex_ref, back_ref):
    chan = conv_ref.shape[1]
    groups = {(0, 0): (0, 1), (0, 1): (2,), (1, 0): (0,), (1, 1): (1, 2)}
    for tap in range(9):
        back_ref[tap * chan : (tap + 1) * chan, :] = conv_ref[tap].astype(F32).T.astype(BF16)
    for u in range(2):
        for p in range(2):
            for s in range(2):
                for t in range(2):
                    row = (2 * u + p) * chan
                    col = (2 * s + t) * chan
                    terms = [conv_ref[3 * a + b].astype(F32) for a in groups[s, p] for b in groups[t, u]]
                    vertex_ref[row : row + chan, col : col + chan] = sum(terms[1:], terms[0]).astype(BF16)


def forward_kernel(
    core_ref, latent_ref, above_ref, below_ref, left_ref, right_ref, wv_ref, cot_ref,
    dec_ref, keep_ref, send_ref, box_ref,
    frame, lhs, mixed, rows, *, scale,
):
    cols, height, chan = latent_ref.shape
    core = core_ref[0]
    pad = lhs.shape[1]
    live = height + 8
    frame[...] = jnp.zeros_like(frame)
    frame[0, 0 : height + 2, :] = left_ref[...].astype(F32)
    frame[cols + 1, 0 : height + 2, :] = right_ref[...].astype(F32)
    above = above_ref[...].astype(F32)
    below = below_ref[...].astype(F32)
    for c in range(cols):
        frame[c + 1, 0:1, :] = above[c : c + 1]
        frame[c + 1, height + 1 : height + 2, :] = below[c : c + 1]
        frame[c + 1, 1 : height + 1, :] = latent_ref[c].astype(F32)
    for c in range(cols + 2):
        low = frame[c, 0:pad, :].astype(BF16)
        high = frame[c, 1 : pad + 1, :].astype(BF16)
        if c <= cols:
            lhs[c, :, 0:chan] = low
            lhs[c, :, chan : 2 * chan] = high
        if c >= 1:
            lhs[c - 1, :, 2 * chan : 3 * chan] = low
            lhs[c - 1, :, 3 * chan : 4 * chan] = high
    mixed[...] = jnp.dot(
        lhs[...].reshape((cols + 1) * pad, 4 * chan), wv_ref[...], preferred_element_type=F32
    ).reshape(cols + 1, pad, 4 * chan)

    def column(f, carry):
        for t in range(2):
            adj = []
            for s in range(2):
                phase = 2 * s + t
                x = mixed[f, 0:live, phase * chan : (phase + 1) * chan]
                square = x * x
                tanh = jnp.tanh(GELU_C * x * (1.0 + GELU_K * square))
                cdf = 0.5 + 0.5 * tanh
                slope = cdf + (0.5 * GELU_C) * x * (1.0 - tanh * tanh) * (
                    1.0 + (3.0 * GELU_K) * square
                )
                dec_ref[phase, f, 0:live, :] = (x * cdf).astype(BF16)
                adj.append(cot_ref[phase, f, 0:live, :].astype(F32) * slope)
            both = adj[0] + adj[1]
            rows[t, f, 0, :, :] = both[1 : height + 1]
            rows[t, f, 1, :, :] = adj[1][0:height] + adj[0][1 : height + 1]
            rows[t, f, 2, :, :] = both[0:height]
        return carry

    lax.fori_loop(0, cols + 1, column, 0)

    def boxes(q, carry):
        at = pl.ds(pl.multiple_of(q * height, height), height)
        for a in range(3):
            first0 = rows[0, q, a]
            first1 = rows[1, q, a]
            next0 = rows[0, q + 1, a]
            next1 = rows[1, q + 1, a]
            for b, value in enumerate((next0 + next1, first1 + next0, first0 + first1)):
                tap = 3 * a + b
                box_ref[at, tap * chan : (tap + 1) * chan] = value.astype(BF16)
        return carry

    lax.fori_loop(0, cols, boxes, 0)
    flat = latent_ref[...].reshape(cols * height, chan)
    for tap in range(9):
        grad = lax.dot_general(
            box_ref[:, tap * chan : (tap + 1) * chan],
            flat,
            (((0,), (0,)), ((), ())),
            preferred_element_type=F32,
        )
        grad = grad * scale
        lat, half, _, size, _ = keep_ref.shape
        for z in range(half):
            for a in range(lat):
                low = (2 * z * lat + a) * size
                high = low + lat * size
                even = grad[low : low + size]
                odd = grad[high : high + size]
                keep_ref[a, z, tap] = jnp.where(core == 0, even, odd).astype(BF16)
                send_ref[a, z, tap] = jnp.where(core == 0, odd, even).astype(BF16)


def backward_kernel(box_ref, w_ref, pull_ref, out_ref):
    cell = jnp.dot(box_ref[...], w_ref[...], preferred_element_type=F32).astype(BF16)
    out_ref[...] = jnp.dot(pull_ref[...], cell, preferred_element_type=F32).astype(BF16)


def reduce_grad(keep, send):
    lat, half, _, size, chan = keep.shape
    lon = 2 * half
    a = lax.axis_index("lat")
    z = lax.axis_index("lon") // 2
    got = lax.ppermute(send, "lon", [(i, i ^ 1) for i in range(lon)])
    pair = (keep.astype(F32) + got.astype(F32)).astype(BF16)
    parts = [lax.ppermute(pick(pair, (a + k) % lat, 0), "lat", shifted("lat", k)) for k in range(1, lat)]
    total = pick(pair, a, 0).astype(F32)
    for part in parts:
        total = total + part.astype(F32)
    total = total.astype(BF16)
    parts = [
        lax.ppermute(pick(total, (z + k) % half, 0), "lon", shifted("lon", 2 * k))
        for k in range(1, half)
    ]
    piece = pick(total, z, 0).astype(F32)
    for part in parts:
        piece = piece + part.astype(F32)
    piece = piece.astype(BF16)
    parts = [piece] + [lax.ppermute(piece, "lat", shifted("lat", k)) for k in range(1, lat)]
    ring = jnp.stack(parts[::-1] * 2)
    ordered = lax.dynamic_slice_in_dim(ring, lat - 1 - a, lat, 0)
    return ordered.transpose(1, 0, 2, 3).reshape(9, lat * size, chan)


def local(tokens, dest_tile, slot_cell, w_up, w_down, w_proj, w_conv, cotangent):
    tok_count = tokens.shape[0]
    tile_count = lax.axis_size("lat") * lax.axis_size("lon")
    capacity = slot_cell.shape[2]
    slots = tile_count * capacity
    rows_fine, cols_fine, chan = cotangent.shape
    height = rows_fine // 2
    width = cols_fine // 2
    cell_count = height * width

    positions = jnp.arange(tok_count, dtype=jnp.int32)
    same_dest = jnp.logical_and(
        dest_tile[:, None] == dest_tile[None, :], positions[None, :] < positions[:, None]
    )
    token_rank = jnp.sum(same_dest.astype(jnp.int32), axis=1)
    target = dest_tile * capacity + token_rank
    selector = (jnp.arange(slots, dtype=jnp.int32)[:, None] == target[None, :]).astype(BF16)
    outgoing = encode(tokens, selector, w_proj, w_up, w_down)

    outgoing, slot_cell, cotangent, w_conv = lax.optimization_barrier(
        (outgoing, slot_cell, cotangent, w_conv)
    )
    arrived = lax.all_to_all(
        outgoing.reshape(tile_count, capacity, chan), ("lat", "lon"), 0, 0, tiled=True
    ).reshape(slots, chan)

    slot_of = slot_cell.reshape(slots)
    flipped = jnp.where(slot_of < cell_count, (slot_of % width) * height + slot_of // width, cell_count)
    cells = jnp.arange(cell_count, dtype=jnp.int32)
    placing = (cells[:, None] == flipped[None, :]).astype(BF16)
    pulling = (flipped[:, None] == cells[None, :]).astype(BF16)
    ocean = jnp.sum(placing, axis=1, dtype=F32).reshape(width, height).T

    wet_fine = jnp.repeat(jnp.repeat(ocean, 2, axis=0), 2, axis=1)[:, :, None].astype(BF16)
    wet_cot = wet_fine * cotangent
    above, below = rim_lat(wet_cot[:1], wet_cot[-1:])
    tall = jnp.concatenate([above, wet_cot, below], axis=0)
    left, right = rim_lon(tall[:, :1], tall[:, -1:])
    framed = jnp.concatenate([left, tall, right], axis=1)
    pad = height + 16
    cot_v = framed.reshape(height + 1, 2, width + 1, 2, chan).transpose(1, 3, 2, 0, 4)
    cot_v = jnp.pad(
        cot_v.reshape(4, width + 1, height + 1, chan), ((0, 0), (0, 0), (0, pad - height - 1), (0, 0))
    )
    vmem = pl.BlockSpec(memory_space=pltpu.VMEM)
    w_vertex, w_back = pl.pallas_call(
        weights_kernel,
        out_shape=(
            jax.ShapeDtypeStruct((4 * chan, 4 * chan), BF16),
            jax.ShapeDtypeStruct((9 * chan, chan), BF16),
        ),
        in_specs=[vmem],
        out_specs=(vmem, vmem),
        name="weights",
    )(w_conv.reshape(9, chan, chan))

    latent = jnp.dot(placing, arrived, preferred_element_type=F32).astype(BF16)
    latent = latent.reshape(width, height, chan)
    above, below = rim_lat(latent[:, 0], latent[:, -1])
    edge = lambda c: jnp.concatenate([above[c][None], latent[c], below[c][None]], axis=0)
    left, right = rim_lon(edge(0), edge(width - 1))

    grad_scale = 1.0 / math.sqrt(rows_fine * cols_fine * tile_count)
    lat = lax.axis_size("lat")
    half = lax.axis_size("lon") // 2
    shares = jax.ShapeDtypeStruct((lat, half, 9, chan // (2 * half * lat), chan), BF16)
    core = (lax.axis_index("lon") % 2).astype(jnp.int32).reshape(1)
    dec_v, keep, send, box = pl.pallas_call(
        partial(forward_kernel, scale=grad_scale),
        out_shape=(
            jax.ShapeDtypeStruct((4, width + 1, pad, chan), BF16),
            shares,
            shares,
            jax.ShapeDtypeStruct((cell_count, 9 * chan), BF16),
        ),
        in_specs=[pl.BlockSpec(memory_space=pltpu.SMEM)] + [vmem] * 7,
        out_specs=(vmem, vmem, vmem, vmem),
        scratch_shapes=[
            pltpu.VMEM((width + 2, pad + 8, chan), F32),
            pltpu.VMEM((width + 1, pad, 4 * chan), BF16),
            pltpu.VMEM((width + 1, pad, 4 * chan), F32),
            pltpu.VMEM((2, width + 1, 3, height, chan), F32),
        ],
        compiler_params=pltpu.CompilerParams(vmem_limit_bytes=56 * 1024 * 1024),
        name="forward",
    )(core, latent, above, below, left, right, w_vertex, cot_v)

    weight_grad = reduce_grad(keep, send)
    block = weight_grad.shape[1]
    weight_grad = weight_grad.astype(F32).reshape(3, 3, block, chan).transpose(0, 1, 3, 2)

    sending = pl.pallas_call(
        backward_kernel,
        out_shape=jax.ShapeDtypeStruct((slots, chan), BF16),
        in_specs=[vmem] * 3,
        out_specs=vmem,
        compiler_params=pltpu.CompilerParams(vmem_limit_bytes=32 * 1024 * 1024),
        name="backward",
    )(box, w_back, pulling)
    returned = lax.all_to_all(
        sending.reshape(tile_count, capacity, chan), ("lat", "lon"), 0, 0, tiled=True
    ).reshape(slots, chan)
    token_grad = lax.dot_general(
        selector, returned, (((0,), (0,)), ((), ())), preferred_element_type=F32
    ).astype(BF16)

    dec = dec_v[:, :, : height + 1].reshape(2, 2, width + 1, height + 1, chan)
    dec = dec.transpose(3, 0, 2, 1, 4).reshape(rows_fine + 2, cols_fine + 2, chan)
    decoded = dec[1:-1, 1:-1] * wet_fine
    return (decoded, weight_grad, token_grad)


def solution(mesh):
    in_specs = (
        P(("lat", "lon"), None),
        P(("lat", "lon")),
        P(("lat", "lon"), None, None),
        P(),
        P(),
        P(),
        P(),
        P("lat", "lon", None),
    )
    out_specs = (P("lat", "lon", None), P(None, None, None, "lon"), P(("lat", "lon"), None))
    return jax.shard_map(local, mesh=mesh, in_specs=in_specs, out_specs=out_specs, check_vma=False)
```
